768 devices in a mesh: dp: 64 (over x, y, core), section: 12 (over z).
Axes of the slice: x: 4, y: 8, z: 12, core: 2. Of those that a mesh axis runs over, the one named last changes fastest.
Arguments:
- hidden_in: bfloat16 [12, 8192, 2048], P('section', 'dp'), may hold values from -80 to 80
- queries: bfloat16 [12, 8192, 2048], P('section', 'dp'), may hold values from -20 to 20
- keys: bfloat16 [12, 8192, 512], P('section', 'dp'), may hold values from -6 to 6
- segments: int32 [64, 128], P('dp'), may hold values from 0 to 3, as said below
- value_weight: bfloat16 [12, 2048, 512], P('section'), may hold values from -0.125 to 0.125
- norm_gain: float32 [12, 2048], P('section'), may hold values from 0.25 to 1.75
- upstream: bfloat16 [8192, 2048], P('dp'), may hold values from -6 to 6
Outputs:
- input_grads: bfloat16 [12, 8192, 2048], P('section', 'dp')
- value_weight_grads: float32 [12, 2048, 512], P('section', 'dp')
- gain_grads: float32 [12, 2048], P('section', 'dp')
The draws below stay inside these ranges and needn't reach their ends.
Inputs may be any that keep to these rules, and one draw needn't show every extreme that they name: `segments`: within each aligned block of 64 list-order tokens of a replica the list ids run from 0 to 3 in order, never falling; each of the 4 lists has 1 to 48 tokens and one has exactly 48.
All inputs are finite; a program needn't handle non-finite values.
Results may differ from the reference program's by a relative error of at most 0.03.
Values may be sent and summed in bfloat16 or wider, within the bound.
A program may use at most 32 MiB of HBM per device.

```python
import math
import jax
import jax.numpy as jnp
from jax import lax

QUERY_HEADS = 16
KEY_VALUE_HEADS = 4
HEAD_FEATURES = 128
D = 2048
KW = 512
MICRO_ROWS = 64
MICRO = 2
LISTS = 4
LIST_MAX = 48
TOK_DEV = 128
REPLICAS = 64
PIECE = 2
TOKEN_COUNT = 8192
LAYER_COUNT = 12


def block_lists(block_key):
    first_key, second_key = jax.random.split(block_key)
    remainder = MICRO_ROWS - LIST_MAX
    cut_points = jnp.sort(jax.random.permutation(first_key, remainder - 1)[:LISTS - 2] + 1).astype(jnp.int32)
    edge_list = jnp.concatenate([jnp.zeros((1,), jnp.int32), cut_points, jnp.full((1,), remainder, jnp.int32)])
    short_lengths = edge_list[1:] - edge_list[:-1]
    position = jax.random.randint(second_key, (), 0, LISTS)
    list_index = jnp.arange(LISTS, dtype=jnp.int32)
    source = jnp.clip(list_index - (list_index > position).astype(jnp.int32), 0, LISTS - 2)
    lengths = jnp.where(list_index == position, LIST_MAX, short_lengths[source]).astype(jnp.int32)
    list_ends = jnp.cumsum(lengths).astype(jnp.int32)
    rows_here = jnp.arange(MICRO_ROWS, dtype=jnp.int32)
    return jnp.sum((rows_here[:, None] >= list_ends[None, :LISTS - 1]).astype(jnp.int32), axis=1)


def list_table(key):
    base_key = jax.random.fold_in(key, 7001)
    block_keys = jax.random.split(base_key, REPLICAS * MICRO)
    return jax.vmap(block_lists)(block_keys).reshape(REPLICAS, TOK_DEV).astype(jnp.int32)


def draw_segments(key, part):
    return list_table(key)


def to_loader(values):
    width = values.shape[-1]
    shaped = values.reshape(LAYER_COUNT, REPLICAS, REPLICAS, PIECE, width)
    return shaped.transpose(0, 2, 1, 3, 4).reshape(LAYER_COUNT, TOKEN_COUNT, width)


def draw_keys(key, part):
    noise_key = jax.random.fold_in(key, 7004)
    target_shape = (LAYER_COUNT, TOKEN_COUNT, KEY_VALUE_HEADS, HEAD_FEATURES)
    values = jnp.clip(jax.random.normal(noise_key, target_shape, jnp.float32), -6.0, 6.0)
    return to_loader(values.reshape(LAYER_COUNT, TOKEN_COUNT, KW)).astype(jnp.bfloat16)


def draw_queries(key, part):
    noise_key = jax.random.fold_in(key, 7005)
    group_width = QUERY_HEADS // KEY_VALUE_HEADS
    target_shape = (LAYER_COUNT, TOKEN_COUNT, KEY_VALUE_HEADS, group_width, HEAD_FEATURES)
    values = jnp.clip(jax.random.normal(noise_key, target_shape, jnp.float32), -6.0, 6.0)
    return to_loader(values.reshape(LAYER_COUNT, TOKEN_COUNT, D)).astype(jnp.bfloat16)


def draw_hidden_in(key, part):
    base_key = jax.random.fold_in(key, 7011)
    row_key = jax.random.fold_in(key, 7012)
    column_key = jax.random.fold_in(key, 7013)
    values = jnp.clip(jax.random.normal(base_key, (LAYER_COUNT, TOKEN_COUNT, D), jnp.float32), -6.0, 6.0)
    row_scale = jnp.exp(jax.random.uniform(row_key, (LAYER_COUNT, TOKEN_COUNT, 1), jnp.float32) * math.log(10.0))
    column_scale = jnp.exp(jax.random.uniform(column_key, (LAYER_COUNT, 1, D), jnp.float32) * math.log(10.0))
    return (values * row_scale * column_scale * 0.1).astype(jnp.bfloat16)


def steps_of(key, shape, cuts, smallest, top_value):
    level = 1.0
    for axis_at, shards_of in cuts:
        heights = jax.random.uniform(jax.random.fold_in(jax.random.fold_in(key, 6), axis_at), (shards_of,), jnp.float32, smallest / len(cuts), top_value / len(cuts))
        level = level * jnp.repeat(jnp.exp(heights), shape[axis_at] // shards_of).reshape((-1,) + (1,) * (len(shape) - 1 - axis_at))
    return level


def normal_values(stream_key, shape, scale, bound, cuts=(), kind=jnp.bfloat16):
    level = steps_of(stream_key, shape, cuts, -0.22, 0.18) if cuts else 1.0
    entries = jax.random.normal(stream_key, shape, jnp.float32) * scale * level
    return jnp.minimum(jnp.maximum(entries, -bound), bound).astype(kind)


def setup_inputs(seed: int = 0) -> dict:
    key_of = jax.random.split(jax.random.key(seed), 8)
    hidden_in = draw_hidden_in(jax.random.fold_in(key_of[7], 71), 0)
    queries = draw_queries(jax.random.fold_in(key_of[7], 71), 0)
    keys = draw_keys(jax.random.fold_in(key_of[7], 71), 0)
    segments = draw_segments(jax.random.fold_in(key_of[7], 71), 0)
    value_weight = normal_values(key_of[4], (LAYER_COUNT, D, KW), D ** -0.5, 0.125, ((0, 12),))
    norm_gain = jnp.clip(1.0 + 0.15 * jax.random.normal(key_of[5], (LAYER_COUNT, D), jnp.float32), 0.25, 1.75)
    upstream = normal_values(key_of[6], (TOKEN_COUNT, D), 1.0, 6.0, ((0, 64),))
    return dict(hidden_in=hidden_in, queries=queries, keys=keys, segments=segments, value_weight=value_weight, norm_gain=norm_gain, upstream=upstream)


epsilon = 1e-06
masked_score = -1e+30

def reorder(rows):
    width = rows.shape[-1]
    return rows.reshape(REPLICAS, REPLICAS, PIECE, width).transpose(1, 0, 2, 3).reshape(TOKEN_COUNT, width)

def block_values(query_tile_block, key_tile_block, gradient_block, list_block):
    group_width = QUERY_HEADS // KEY_VALUE_HEADS
    query_grid4 = query_tile_block.astype(jnp.float32).reshape(MICRO_ROWS, KEY_VALUE_HEADS, group_width, HEAD_FEATURES)
    key_grid3 = key_tile_block.astype(jnp.float32).reshape(MICRO_ROWS, KEY_VALUE_HEADS, HEAD_FEATURES)
    scores = jnp.einsum('ikgd,jkd->kgij', query_grid4, key_grid3) * HEAD_FEATURES ** (-0.5)
    positions = jnp.arange(MICRO_ROWS, dtype=jnp.int32)
    allowed = (list_block[:, None] == list_block[None, :]) & (positions[None, :] <= positions[:, None])
    scores = jnp.where(allowed, scores, masked_score)
    exp_scores = jnp.exp(scores - lax.optimization_barrier(jnp.max(scores, axis=-1, keepdims=True)))
    block_weights = (exp_scores / lax.optimization_barrier(jnp.sum(exp_scores, axis=-1, keepdims=True))).astype(jnp.bfloat16)
    gradient_grid4 = gradient_block.astype(jnp.float32).reshape(MICRO_ROWS, KEY_VALUE_HEADS, group_width, HEAD_FEATURES)
    value_gradient = jnp.einsum('kgij,ikgd->jkd', block_weights.astype(jnp.float32), gradient_grid4)
    return value_gradient.reshape(MICRO_ROWS, KEY_VALUE_HEADS * HEAD_FEATURES).astype(jnp.bfloat16)

def block_entry(inputs):
    return block_values(inputs[0], inputs[1], inputs[2], inputs[3])

def reference(hidden_in, queries, keys, segments, value_weight, norm_gain, upstream):
    block_count = TOKEN_COUNT // MICRO_ROWS
    list_blocks = segments.reshape(block_count, MICRO_ROWS)
    scale_total = TOKEN_COUNT ** (-0.5)
    grad_now = upstream
    input_list = []
    weight_list = []
    gain_list = []
    for layer_index in range(LAYER_COUNT - 1, -1, -1):
        x_wide = reorder(hidden_in[layer_index]).astype(jnp.float32)
        inv_rms = lax.rsqrt(lax.optimization_barrier(jnp.mean(x_wide * x_wide, axis=1, keepdims=True)) + epsilon)
        x_norm = x_wide * inv_rms
        gain_row = norm_gain[layer_index]
        normed = (x_norm * gain_row).astype(jnp.bfloat16)
        inputs = (reorder(queries[layer_index]).reshape(block_count, MICRO_ROWS, D), reorder(keys[layer_index]).reshape(block_count, MICRO_ROWS, KW), grad_now.reshape(block_count, MICRO_ROWS, D), list_blocks)
        value_gradient = lax.map(block_entry, inputs).reshape(TOKEN_COUNT, KW)
        normed_grad = jnp.dot(value_gradient, value_weight[layer_index].T, preferred_element_type=jnp.float32)
        scaled = normed_grad * gain_row
        inner_mean = lax.optimization_barrier(jnp.mean(x_norm * scaled, axis=1, keepdims=True))
        input_grad = (grad_now.astype(jnp.float32) + inv_rms * (scaled - x_norm * inner_mean)).astype(jnp.bfloat16)
        weight_grad = jnp.dot(normed.T, value_gradient, preferred_element_type=jnp.float32) * scale_total
        gain_grad = lax.optimization_barrier(jnp.sum(x_norm * normed_grad, axis=0)) * scale_total
        input_list.append(reorder(input_grad))
        weight_list.append(weight_grad)
        gain_list.append(gain_grad)
        grad_now = input_grad
    return (jnp.stack(input_list[::-1]), jnp.stack(weight_list[::-1]), jnp.stack(gain_list[::-1]))
```

```python
import functools

import jax
import jax.numpy as jnp
from jax import lax
from jax.experimental import pallas as pl
from jax.experimental.pallas import tpu as pltpu
from jax.sharding import PartitionSpec as P

HEADS = 16
KV = 4
GROUP = HEADS // KV
HF = 128
D = HEADS * HF
KW = KV * HF
ROWS = 64
MICRO = 2
TOK = ROWS * MICRO
PR = 16
PIECES = TOK // PR
PER = ROWS // PR
EPS = 1e-06
MASKED = -1e30
XS = 4
MESH = pl.DeviceIdType.MESH
F32 = jnp.float32
BF = jnp.bfloat16


def dot(a, b, dims=(((1,), (0,)), ((), ()))):
    return lax.dot_general(a, b, dims, preferred_element_type=F32)


NT = (((1,), (1,)), ((), ()))


def rows_of(i, n):
    return pl.ds(pl.multiple_of(i * n, n), n)


def kernel(
    nx, ny, nz,
    x_ref, q_ref, k_ref, segc_ref, segr_ref, w_ref, gain_ref, up_ref,
    out_ref, csum_ref,
    gin, gs, pt, yv, inv, wt, xs, xst, us, cst, part,
    up_sem, gin_sem, gout_sem, xs_recv, xs_send, us_recv, us_send, part_recv, part_send,
):
    me = lax.axis_index("dp")
    sec = lax.axis_index("section")
    core = lax.rem(me, 2)
    my_y = lax.rem(lax.div(me, 2), ny)
    my_x = lax.div(me, 2 * ny)
    last = nz - 1
    slots = 2 * nx
    fw = D // slots
    fo = D // (2 * nx * ny)
    slot = my_x * 2 + core

    def dev(x, y, c):
        return (x * ny + y) * 2 + c

    barrier = pltpu.get_barrier_semaphore()
    total = 0
    for dx in range(nx):
        for dy in range(ny):
            for dc in range(2):
                if (dx == 0 or dy == 0) and dx + dy + dc > 0:
                    target = dev(
                        lax.rem(my_x + dx, nx), lax.rem(my_y + dy, ny), lax.rem(core + dc, 2)
                    )
                    pl.semaphore_signal(
                        barrier, inc=1, device_id=(target, sec), device_id_type=MESH
                    )
                    total += 1

    @pl.when(sec > 0)
    def _():
        pl.semaphore_signal(barrier, inc=1, device_id=(me, sec - 1), device_id_type=MESH)

    @pl.when(sec < last)
    def _():
        pl.semaphore_signal(barrier, inc=1, device_id=(me, sec + 1), device_id_type=MESH)

    up_copy = pltpu.make_async_copy(up_ref, gin, up_sem)

    @pl.when(sec == last)
    def _():
        up_copy.start()

    gain = gain_ref[...]

    @pl.loop(0, PIECES)
    def _(i):
        xf = x_ref[rows_of(i, PR), :].astype(F32)
        r = lax.rsqrt(jnp.sum(xf * xf, axis=1, keepdims=True) * (1.0 / D) + EPS)
        inv[rows_of(i, PR), :] = r

    xg = (x_ref[...].astype(F32) * gain).astype(BF)
    yv[...] = dot(xg, w_ref[...]) * (1.0 / D)
    gs[...] = jnp.zeros_like(gs)

    def probs(m, _):
        segc = segc_ref[rows_of(m, ROWS), :]
        segr = segr_ref[m]
        j = lax.broadcasted_iota(jnp.int32, (ROWS, GROUP * ROWS), 0)
        i = lax.rem(lax.broadcasted_iota(jnp.int32, (ROWS, GROUP * ROWS), 1), ROWS)
        allowed = (segc == segr) & (j <= i)
        for c in range(KV):
            kc = k_ref[rows_of(m, ROWS), c * HF:(c + 1) * HF]
            qc = jnp.concatenate(
                [
                    q_ref[rows_of(m, ROWS), (c * GROUP + h) * HF:(c * GROUP + h + 1) * HF]
                    for h in range(GROUP)
                ],
                axis=0,
            )
            s = dot(kc, qc, NT) * HF ** (-0.5)
            s = jnp.where(allowed, s, MASKED)
            e = jnp.exp(s - jnp.max(s, axis=0, keepdims=True))
            pt[m, c] = (e / jnp.sum(e, axis=0, keepdims=True)).astype(BF)
        return 0

    lax.fori_loop(0, MICRO, probs, 0)

    for i in range(D // HF):
        wt[:, i * HF:(i + 1) * HF] = w_ref[i * HF:(i + 1) * HF, :].T

    neighbours = (sec > 0).astype(jnp.int32) + (sec < last).astype(jnp.int32)
    pl.semaphore_wait(barrier, total + neighbours)

    def peer(step):
        p = lax.rem(slot + step, slots)
        px = lax.div(p, 2)
        pc = lax.rem(p, 2)
        return p, dev(px, my_y, pc)

    def x_copy(step):
        p, target = peer(step)
        return pltpu.make_async_remote_copy(
            src_ref=x_ref.at[:, pl.ds(pl.multiple_of(p * fw, fw), fw)],
            dst_ref=xs.at[slot],
            send_sem=xs_send.at[step],
            recv_sem=xs_recv,
            device_id=(target, sec),
            device_id_type=MESH,
        )

    for step in range(1, slots):
        x_copy(step).start()
    own_x = pltpu.make_async_copy(
        x_ref.at[:, pl.ds(pl.multiple_of(slot * fw, fw), fw)], xs.at[slot], xs_recv
    )
    own_x.start()

    def turn_x():
        pltpu.make_async_copy(xs, xs, xs_recv).wait()
        for i in range(slots):
            xst[:, i * TOK:(i + 1) * TOK] = xs[i].T

    @pl.when(sec < last)
    def _():
        turn_x()

    @pl.when(sec == last)
    def _():
        up_copy.wait()

    def g_copy(ci):
        return pltpu.make_async_remote_copy(
            src_ref=out_ref.at[ci],
            dst_ref=gin.at[ci],
            send_sem=gout_sem.at[ci],
            recv_sem=gin_sem.at[ci],
            device_id=(me, lax.max(sec - 1, 0)),
            device_id_type=MESH,
        )

    def u_copy(ci, step):
        p, target = peer(step)
        return pltpu.make_async_remote_copy(
            src_ref=us.at[slot, rows_of(ci, PR), :],
            dst_ref=us.at[slot, rows_of(ci, PR), :],
            send_sem=us_send.at[ci, step],
            recv_sem=us_recv,
            device_id=(target, sec),
            device_id_type=MESH,
        )

    def chain(t, _):
        m = lax.rem(t, MICRO)
        b = PER - 1 - lax.div(t, MICRO)
        ci = m * PER + b

        @pl.when(sec < last)
        def _():
            pltpu.make_async_copy(out_ref.at[ci], gin.at[ci], gin_sem.at[ci]).wait()

        g = gin[ci]
        for h in range(HEADS):
            c, hh = divmod(h, GROUP)
            gs[m, c, pl.ds(pl.multiple_of(hh * ROWS + b * PR, PR), PR), :] = g[:, h * HF:(h + 1) * HF]
        v = jnp.concatenate(
            [dot(pt[m, c, rows_of(b, PR), :], gs[m, c]) for c in range(KV)], axis=1
        ).astype(BF)
        r = inv[rows_of(ci, PR), :]
        uf = v.astype(F32) * r
        u = uf.astype(BF)
        coef = jnp.sum(uf * yv[rows_of(ci, PR), :], axis=1, keepdims=True) * (r * r)
        ng = dot(u, wt[...])
        xf = x_ref[rows_of(ci, PR), :].astype(F32)
        out_ref[ci] = (g.astype(F32) + (gain * ng - xf * coef)).astype(BF)

        @pl.when(sec > 0)
        def _():
            g_copy(ci).start()

        us[slot, rows_of(ci, PR), :] = u
        for step in range(1, slots):
            u_copy(ci, step).start()
        return 0

    lax.fori_loop(0, PIECES, chain, 0)

    @pl.when(sec == last)
    def _():
        turn_x()

    others = us.at[pl.ds(0, slots - 1)]
    pltpu.make_async_copy(others, others, us_recv).wait()
    acc = dot(xst[...], us[...].reshape(slots * TOK, KW))
    cst[...] = acc.astype(BF).reshape(ny, fo, KW)

    def part_copy(j):
        yl, c = divmod(j, 2)
        target = dev(my_x, core * (ny // 2) + yl, c)
        return target, pltpu.make_async_remote_copy(
            src_ref=cst.at[j],
            dst_ref=part.at[my_y],
            send_sem=part_send.at[j],
            recv_sem=part_recv,
            device_id=(target, sec),
            device_id_type=MESH,
        )

    for j in range(ny):
        target, copy = part_copy(j)

        @pl.when(target != me)
        def _():
            copy.start()

        @pl.when(target == me)
        def _():
            pltpu.make_async_copy(cst.at[j], part.at[my_y], part_recv).start()

    pltpu.make_async_copy(part, part, part_recv).wait()
    total_c = part[0].astype(F32)
    for y in range(1, ny):
        total_c = total_c + part[y].astype(F32)
    csum_ref[...] = total_c

    for step in range(1, slots):
        x_copy(step).wait_send()
    def drain(ci, _):
        for step in range(1, slots):
            u_copy(ci, step).wait_send()

        @pl.when(sec > 0)
        def _():
            g_copy(ci).wait_send()

        return 0

    lax.fori_loop(0, PIECES, drain, 0)
    for j in range(ny):
        target, copy = part_copy(j)

        @pl.when(target != me)
        def _():
            copy.wait_send()


def backward(nx, ny, nz, x, q, k, segc, segr, w, gain, up):
    slots = 2 * nx
    fw = D // slots
    fo = D // (2 * nx * ny)
    vmem = pl.BlockSpec(memory_space=pltpu.VMEM)
    sem = pltpu.SemaphoreType.DMA
    return pl.pallas_call(
        functools.partial(kernel, nx, ny, nz),
        out_shape=(
            jax.ShapeDtypeStruct((PIECES, PR, D), BF),
            jax.ShapeDtypeStruct((fo, KW), F32),
        ),
        in_specs=[vmem] * 7 + [pl.BlockSpec(memory_space=pl.ANY)],
        out_specs=(vmem, vmem),
        scratch_shapes=[
            pltpu.VMEM((PIECES, PR, D), BF),
            pltpu.VMEM((MICRO, KV, GROUP * ROWS, HF), BF),
            pltpu.VMEM((MICRO, KV, ROWS, GROUP * ROWS), BF),
            pltpu.VMEM((TOK, KW), F32),
            pltpu.VMEM((TOK, 1), F32),
            pltpu.VMEM((KW, D), BF),
            pltpu.VMEM((slots, TOK, fw), BF),
            pltpu.VMEM((fw, slots * TOK), BF),
            pltpu.VMEM((slots, TOK, KW), BF),
            pltpu.VMEM((ny, fo, KW), BF),
            pltpu.VMEM((ny, fo, KW), BF),
            sem,
            sem((PIECES,)),
            sem((PIECES,)),
            sem,
            sem((slots,)),
            sem,
            sem((PIECES, slots)),
            sem,
            sem((ny,)),
        ],
        compiler_params=pltpu.CompilerParams(collective_id=0, has_side_effects=True, vmem_limit_bytes=60000 * 1024),
        name="chain",
    )(x, q, k, segc, segr, w, gain, up)


def on_device(nx, ny, nz, hidden_in, queries, keys, segments, value_weight, norm_gain, upstream):
    regroup = functools.partial(
        lax.all_to_all, axis_name="dp", split_axis=1, concat_axis=1, tiled=True
    )
    k = regroup(keys)[0]
    q = regroup(queries)[0]
    x = regroup(hidden_in)[0]
    segc = segments.reshape(TOK, 1)
    segr = jnp.tile(segments.reshape(MICRO, 1, ROWS), (1, 1, GROUP))
    w = value_weight[0]
    out, csum = backward(
        nx, ny, nz, x, q, k, segc, segr, w, norm_gain, upstream.reshape(PIECES, PR, D)
    )
    stored = lax.all_to_all(out.reshape(TOK, D), "dp", split_axis=0, concat_axis=0, tiled=True)
    fo = csum.shape[0]
    scale = float(TOK * 2 * nx * ny) ** (-0.5)
    start = lax.axis_index("dp") * fo
    own_gain = lax.dynamic_slice_in_dim(norm_gain[0], start, fo, 0)
    own_w = lax.dynamic_slice_in_dim(w, start, fo, 0).astype(F32)
    weight = csum * (own_gain[:, None] * scale)
    gains = jnp.sum(csum * own_w, axis=1) * scale
    return stored[None], weight[None], gains[None]


def solution(mesh):
    ndp = mesh.shape["dp"]
    nx = XS
    ny = ndp // (2 * nx)
    in_specs = (
        P("section", "dp", None),
        P("section", "dp", None),
        P("section", "dp", None),
        P("dp", None),
        P("section", None, None),
        P("section", None),
        P("dp", None),
    )
    out_specs = (P("section", "dp", None), P("section", "dp", None), P("section", "dp"))
    return jax.shard_map(
        functools.partial(on_device, nx, ny, mesh.shape["section"]),
        mesh=mesh, in_specs=in_specs, out_specs=out_specs, check_vma=False,
    )
```

```python
import functools

import jax
import jax.numpy as jnp
from jax import lax
from jax.experimental import pallas as pl
from jax.experimental.pallas import tpu as pltpu
from jax.sharding import PartitionSpec as P

HEADS = 16
KV = 4
GROUP = HEADS // KV
HF = 128
D = HEADS * HF
KW = KV * HF
ROWS = 64
MICRO = 2
TOK = ROWS * MICRO
PR = 16
PIECES = TOK // PR
PER = ROWS // PR
EPS = 1e-06
MASKED = -1e30
XS = 4
MESH = pl.DeviceIdType.MESH
F32 = jnp.float32
BF = jnp.bfloat16


def dot(a, b, dims=(((1,), (0,)), ((), ()))):
    return lax.dot_general(a, b, dims, preferred_element_type=F32)


NT = (((1,), (1,)), ((), ()))


def rows_of(i, n):
    return pl.ds(pl.multiple_of(i * n, n), n)


def kernel(
    nx, ny, nz,
    x_in, q_in, k_in, seg_ref, w_ref, gain_ref, up_ref,
    fin_ref, wg_ref, gg_ref,
    ql, kl, xl, out, gin, gs, mask, pt, yv, inv, wt, xs, xst, us, cst, part, gcol, spare,
    up_sem, list_recv, list_send, gin_sem, gout_sem, fin_recv, fin_send,
    xs_recv, xs_send, us_recv, us_send, part_recv, part_send,
):
    me = lax.axis_index("dp")
    sec = lax.axis_index("section")
    core = lax.rem(me, 2)
    my_y = lax.rem(lax.div(me, 2), ny)
    my_x = lax.div(me, 2 * ny)
    last = nz - 1
    ndp = 2 * nx * ny
    pair = TOK // ndp
    slots = 2 * nx
    fw = D // slots
    fo = D // ndp
    slot = my_x * 2 + core
    scale = float(TOK * ndp) ** (-0.5)

    def dev(x, y, c):
        return (x * ny + y) * 2 + c

    def remote(src, dst, send, recv, target, section=None):
        return pltpu.make_async_remote_copy(
            src_ref=src, dst_ref=dst, send_sem=send, recv_sem=recv,
            device_id=(target, sec if section is None else section), device_id_type=MESH,
        )

    barrier = pltpu.get_barrier_semaphore()

    def greet(d, _):
        pl.semaphore_signal(
            barrier, inc=1, device_id=(lax.rem(me + d, ndp), sec), device_id_type=MESH
        )
        return 0

    lax.fori_loop(1, ndp, greet, 0)

    @pl.when(sec > 0)
    def _():
        pl.semaphore_signal(barrier, inc=1, device_id=(me, sec - 1), device_id_type=MESH)

    @pl.when(sec < last)
    def _():
        pl.semaphore_signal(barrier, inc=1, device_id=(me, sec + 1), device_id_type=MESH)

    up_copy = pltpu.make_async_copy(up_ref, gin, up_sem)

    @pl.when(sec == last)
    def _():
        up_copy.start()

    neighbours = (sec > 0).astype(jnp.int32) + (sec < last).astype(jnp.int32)
    pl.semaphore_wait(barrier, ndp - 1 + neighbours)

    arrays = ((k_in, kl), (q_in, ql), (x_in, xl))
    for n, (src, dst) in enumerate(arrays):

        def give(d, _):
            target = lax.rem(me + d, ndp)
            remote(
                src.at[rows_of(target, pair), :], dst.at[rows_of(me, pair), :],
                list_send.at[n], list_recv.at[n], target,
            ).start()
            return 0

        lax.fori_loop(1, ndp, give, 0)
        pltpu.make_async_copy(
            src.at[rows_of(me, pair), :], dst.at[rows_of(me, pair), :], list_recv.at[n]
        ).start()
        pltpu.make_async_copy(
            src.at[rows_of(me, pair), :],
            spare.at[n, pl.ds(0, pair), pl.ds(0, src.shape[1])],
            list_send.at[n],
        ).start()

    def listed(n):
        pltpu.make_async_copy(arrays[n][1], arrays[n][1], list_recv.at[n]).wait()

    gain = gain_ref[...]
    segs = jnp.broadcast_to(seg_ref[...].astype(F32), (GROUP * ROWS, TOK)).astype(BF)

    def lane(shape, axis):
        return lax.broadcasted_iota(jnp.int32, shape, axis)

    for m in range(MICRO):
        pick = (lane((ROWS, TOK), 0) + m * ROWS == lane((ROWS, TOK), 1)).astype(F32).astype(BF)
        key_list = dot(pick, segs, NT)
        wide = (TOK, GROUP * ROWS)
        spread = (lane(wide, 0) == lax.rem(lane(wide, 1), ROWS) + m * ROWS).astype(F32).astype(BF)
        query_list = dot(segs[:ROWS], spread)
        tall = (ROWS, GROUP * ROWS)
        causal = lane(tall, 0) <= lax.rem(lane(tall, 1), ROWS)
        mask[m] = jnp.where((key_list == query_list) & causal, 1.0, 0.0)
    for i in range(D // HF):
        wt[:, i * HF:(i + 1) * HF] = w_ref[i * HF:(i + 1) * HF, :].T
    own = lane((fo, D), 1) == me * fo + lane((fo, D), 0)
    gcol[...] = jnp.sum(jnp.where(own, gain, 0.0), axis=1, keepdims=True)
    gs[...] = jnp.zeros_like(gs)

    listed(0)
    listed(1)

    def probs(m, _):
        allowed = mask[m] > 0.5
        for c in range(KV):
            kc = kl[rows_of(m, ROWS), c * HF:(c + 1) * HF]
            qc = jnp.concatenate(
                [
                    ql[rows_of(m, ROWS), (c * GROUP + h) * HF:(c * GROUP + h + 1) * HF]
                    for h in range(GROUP)
                ],
                axis=0,
            )
            s = dot(kc, qc, NT) * HF ** (-0.5)
            s = jnp.where(allowed, s, MASKED)
            e = jnp.exp(s - jnp.max(s, axis=0, keepdims=True))
            pt[m, c] = (e / jnp.sum(e, axis=0, keepdims=True)).astype(BF)
        return 0

    lax.fori_loop(0, MICRO, probs, 0)

    listed(2)

    def peer(step):
        p = lax.rem(slot + step, slots)
        return p, dev(lax.div(p, 2), my_y, lax.rem(p, 2))

    def columns(p):
        return xl.at[:, pl.ds(pl.multiple_of(p * fw, fw), fw)]

    def x_copy(step):
        p, target = peer(step)
        return remote(columns(p), xs.at[slot], xs_send.at[step], xs_recv, target)

    for step in range(1, slots):
        x_copy(step).start()
    pltpu.make_async_copy(columns(slot), xs.at[slot], xs_recv).start()

    def stats(i, _):
        xf = xl[rows_of(i, PR), :].astype(F32)
        inv[rows_of(i, PR), :] = lax.rsqrt(
            jnp.sum(xf * xf, axis=1, keepdims=True) * (1.0 / D) + EPS
        )
        return 0

    lax.fori_loop(0, PIECES, stats, 0)
    xg = (xl[...].astype(F32) * gain).astype(BF)
    yv[...] = dot(xg, w_ref[...]) * (1.0 / D)

    def turn_x():
        pltpu.make_async_copy(xs, xs, xs_recv).wait()
        for i in range(slots):
            xst[:, i * TOK:(i + 1) * TOK] = xs[i].T

    @pl.when(sec < last)
    def _():
        turn_x()

    @pl.when(sec == last)
    def _():
        up_copy.wait()

    def g_copy(ci):
        return remote(
            out.at[rows_of(ci, PR), :], gin.at[rows_of(ci, PR), :],
            gout_sem.at[ci], gin_sem.at[ci], me, lax.max(sec - 1, 0),
        )

    def u_copy(ci, step):
        _, target = peer(step)
        rows = us.at[slot, rows_of(ci, PR), :]
        return remote(rows, rows, us_send.at[ci, step], us_recv, target)

    def chain(t, _):
        m = lax.rem(t, MICRO)
        b = PER - 1 - lax.div(t, MICRO)
        ci = m * PER + b

        @pl.when(sec < last)
        def _():
            g_copy(ci).wait_recv()

        g = gin[rows_of(ci, PR), :]
        for h in range(HEADS):
            c, hh = divmod(h, GROUP)
            gs[m, c, pl.ds(pl.multiple_of(hh * ROWS + b * PR, PR), PR), :] = g[:, h * HF:(h + 1) * HF]
        v = jnp.concatenate(
            [dot(pt[m, c, rows_of(b, PR), :], gs[m, c]) for c in range(KV)], axis=1
        ).astype(BF)
        r = inv[rows_of(ci, PR), :]
        uf = v.astype(F32) * r
        u = uf.astype(BF)
        coef = jnp.sum(uf * yv[rows_of(ci, PR), :], axis=1, keepdims=True) * (r * r)
        ng = dot(u, wt[...])
        xf = xl[rows_of(ci, PR), :].astype(F32)
        out[rows_of(ci, PR), :] = (g.astype(F32) + (gain * ng - xf * coef)).astype(BF)
        us[slot, rows_of(ci, PR), :] = u

        @pl.when(sec > 0)
        def _():
            g_copy(ci).start()

        for step in range(1, slots):
            u_copy(ci, step).start()

        def back(i, _):
            target = ci * (PR // pair) + i
            src = out.at[rows_of(target, pair), :]
            dst = fin_ref.at[rows_of(me, pair), :]

            @pl.when(target != me)
            def _():
                remote(src, dst, fin_send, fin_recv, target).start()

            @pl.when(target == me)
            def _():
                pltpu.make_async_copy(src, dst, fin_recv).start()
                pltpu.make_async_copy(src, spare.at[3, pl.ds(0, pair), :], fin_send).start()

            return 0

        lax.fori_loop(0, PR // pair, back, 0)
        return 0

    lax.fori_loop(0, PIECES, chain, 0)

    @pl.when(sec == last)
    def _():
        turn_x()

    others = us.at[pl.ds(0, slots - 1)]
    pltpu.make_async_copy(others, others, us_recv).wait()
    acc = dot(xst[...], us[...].reshape(slots * TOK, KW))
    cst[...] = acc.astype(BF).reshape(ny, fo, KW)

    def part_copy(j):
        yl, c = divmod(j, 2)
        target = dev(my_x, core * (ny // 2) + yl, c)
        return target, remote(cst.at[j], part.at[my_y], part_send.at[j], part_recv, target)

    for j in range(ny):
        target, copy = part_copy(j)

        @pl.when(target != me)
        def _():
            copy.start()

        @pl.when(target == me)
        def _():
            pltpu.make_async_copy(cst.at[j], part.at[my_y], part_recv).start()

    pltpu.make_async_copy(part, part, part_recv).wait()
    total = part[0].astype(F32)
    for y in range(1, ny):
        total = total + part[y].astype(F32)
    total = total * scale
    wg_ref[...] = total * gcol[...]
    terms = total * w_ref[rows_of(me, fo), :].astype(F32)
    gg_ref[...] = jnp.sum(terms.T, axis=0, keepdims=True)

    pltpu.make_async_copy(fin_ref, fin_ref, fin_recv).wait()

    pltpu.make_async_copy(out, out, fin_send).wait()
    for n, (_, dst) in enumerate(arrays):
        pltpu.make_async_copy(dst, dst, list_send.at[n]).wait()
    for step in range(1, slots):
        x_copy(step).wait_send()

    def drain(ci, _):
        for step in range(1, slots):
            u_copy(ci, step).wait_send()

        @pl.when(sec > 0)
        def _():
            g_copy(ci).wait_send()

        return 0

    lax.fori_loop(0, PIECES, drain, 0)
    for j in range(ny):
        target, copy = part_copy(j)

        @pl.when(target != me)
        def _():
            copy.wait_send()


def on_device(nx, ny, nz, hidden_in, queries, keys, segments, value_weight, norm_gain, upstream):
    slots = 2 * nx
    ndp = slots * ny
    fw = D // slots
    fo = D // ndp
    pair = TOK // ndp
    vmem = pl.BlockSpec(memory_space=pltpu.VMEM)
    hbm = pl.BlockSpec(memory_space=pl.ANY)
    sem = pltpu.SemaphoreType.DMA
    fin, wg, gg = pl.pallas_call(
        functools.partial(kernel, nx, ny, nz),
        out_shape=(
            jax.ShapeDtypeStruct((TOK, D), BF),
            jax.ShapeDtypeStruct((fo, KW), F32),
            jax.ShapeDtypeStruct((1, fo), F32),
        ),
        in_specs=[hbm] * 3 + [vmem] * 3 + [hbm],
        out_specs=(vmem, vmem, vmem),
        scratch_shapes=[
            pltpu.VMEM((TOK, D), BF),
            pltpu.VMEM((TOK, KW), BF),
            pltpu.VMEM((TOK, D), BF),
            pltpu.VMEM((TOK, D), BF),
            pltpu.VMEM((TOK, D), BF),
            pltpu.VMEM((MICRO, KV, GROUP * ROWS, HF), BF),
            pltpu.VMEM((MICRO, ROWS, GROUP * ROWS), F32),
            pltpu.VMEM((MICRO, KV, ROWS, GROUP * ROWS), BF),
            pltpu.VMEM((TOK, KW), F32),
            pltpu.VMEM((TOK, 1), F32),
            pltpu.VMEM((KW, D), BF),
            pltpu.VMEM((slots, TOK, fw), BF),
            pltpu.VMEM((fw, slots * TOK), BF),
            pltpu.VMEM((slots, TOK, KW), BF),
            pltpu.VMEM((ny, fo, KW), BF),
            pltpu.VMEM((ny, fo, KW), BF),
            pltpu.VMEM((fo, 1), F32),
            pltpu.VMEM((4, max(pair, 16), D), BF),
            sem,
            sem((3,)),
            sem((3,)),
            sem((PIECES,)),
            sem((PIECES,)),
            sem,
            sem,
            sem,
            sem((slots,)),
            sem,
            sem((PIECES, slots)),
            sem,
            sem((ny,)),
        ],
        compiler_params=pltpu.CompilerParams(
            collective_id=0, has_side_effects=True, vmem_limit_bytes=60000 * 1024
        ),
        name="chain",
    )(
        hidden_in[0], queries[0], keys[0], segments, value_weight[0], norm_gain, upstream
    )
    return fin[None], wg[None], gg


def solution(mesh):
    ndp = mesh.shape["dp"]
    nx = XS
    ny = ndp // (2 * nx)
    in_specs = (
        P("section", "dp", None),
        P("section", "dp", None),
        P("section", "dp", None),
        P("dp", None),
        P("section", None, None),
        P("section", None),
        P("dp", None),
    )
    out_specs = (P("section", "dp", None), P("section", "dp", None), P("section", "dp"))
    return jax.shard_map(
        functools.partial(on_device, nx, ny, mesh.shape["section"]),
        mesh=mesh, in_specs=in_specs, out_specs=out_specs, check_vma=False,
    )
```

```python
import functools

import jax
import jax.numpy as jnp
from jax import lax
from jax.experimental import pallas as pl
from jax.experimental.pallas import tpu as pltpu
from jax.sharding import PartitionSpec as P

HEADS = 16
KV = 4
GROUP = HEADS // KV
HF = 128
D = HEADS * HF
KW = KV * HF
ROWS = 64
MICRO = 2
TOK = ROWS * MICRO
PR = 8
PIECES = TOK // PR
PER = ROWS // PR
EPS = 1e-06
MASKED = -1e30
XS = 4
MESH = pl.DeviceIdType.MESH
F32 = jnp.float32
BF = jnp.bfloat16


def dot(a, b, dims=(((1,), (0,)), ((), ()))):
    return lax.dot_general(a, b, dims, preferred_element_type=F32)


NT = (((1,), (1,)), ((), ()))


def rows_of(i, n):
    return pl.ds(pl.multiple_of(i * n, n), n)


def kernel(
    nx, ny, nz,
    x_in, q_in, k_in, seg_ref, w_ref, gain_ref, up_ref,
    fin_ref, wg_ref, gg_ref,
    ql, kl, xl, out, gin, gs, mask, pt, yv, inv, wt, xs, xst, us, cst, part, gcol, spare,
    up_sem, list_recv, list_send, gin_sem, gout_sem, fin_recv, fin_send,
    xs_recv, xs_send, us_recv, us_send, part_recv, part_send,
):
    me = lax.axis_index("dp")
    sec = lax.axis_index("section")
    core = lax.rem(me, 2)
    my_y = lax.rem(lax.div(me, 2), ny)
    my_x = lax.div(me, 2 * ny)
    last = nz - 1
    ndp = 2 * nx * ny
    pair = TOK // ndp
    slots = 2 * nx
    fw = D // slots
    fo = D // ndp
    slot = my_x * 2 + core
    scale = float(TOK * ndp) ** (-0.5)

    def dev(x, y, c):
        return (x * ny + y) * 2 + c

    def remote(src, dst, send, recv, target, section=None):
        return pltpu.make_async_remote_copy(
            src_ref=src, dst_ref=dst, send_sem=send, recv_sem=recv,
            device_id=(target, sec if section is None else section), device_id_type=MESH,
        )

    barrier = pltpu.get_barrier_semaphore()

    def greet(d, _):
        pl.semaphore_signal(
            barrier, inc=1, device_id=(lax.rem(me + d, ndp), sec), device_id_type=MESH
        )
        return 0

    lax.fori_loop(1, ndp, greet, 0)

    @pl.when(sec > 0)
    def _():
        pl.semaphore_signal(barrier, inc=1, device_id=(me, sec - 1), device_id_type=MESH)

    @pl.when(sec < last)
    def _():
        pl.semaphore_signal(barrier, inc=1, device_id=(me, sec + 1), device_id_type=MESH)

    up_copy = pltpu.make_async_copy(up_ref, gin, up_sem)

    @pl.when(sec == last)
    def _():
        up_copy.start()

    neighbours = (sec > 0).astype(jnp.int32) + (sec < last).astype(jnp.int32)
    pl.semaphore_wait(barrier, ndp - 1 + neighbours)

    arrays = ((k_in, kl), (q_in, ql), (x_in, xl))
    for n, (src, dst) in enumerate(arrays):

        def give(d, _):
            target = lax.rem(me + d, ndp)
            remote(
                src.at[rows_of(target, pair), :], dst.at[rows_of(me, pair), :],
                list_send.at[n], list_recv.at[n], target,
            ).start()
            return 0

        lax.fori_loop(1, ndp, give, 0)
        pltpu.make_async_copy(
            src.at[rows_of(me, pair), :], dst.at[rows_of(me, pair), :], list_recv.at[n]
        ).start()
        pltpu.make_async_copy(
            src.at[rows_of(me, pair), :],
            spare.at[n, pl.ds(0, pair), pl.ds(0, src.shape[1])],
            list_send.at[n],
        ).start()

    def listed(n):
        pltpu.make_async_copy(arrays[n][1], arrays[n][1], list_recv.at[n]).wait()

    gain = gain_ref[...]
    segs = jnp.broadcast_to(seg_ref[...].astype(F32), (GROUP * ROWS, TOK)).astype(BF)

    def lane(shape, axis):
        return lax.broadcasted_iota(jnp.int32, shape, axis)

    for m in range(MICRO):
        pick = (lane((ROWS, TOK), 0) + m * ROWS == lane((ROWS, TOK), 1)).astype(F32).astype(BF)
        key_list = dot(pick, segs, NT)
        wide = (TOK, GROUP * ROWS)
        spread = (lane(wide, 0) == lax.rem(lane(wide, 1), ROWS) + m * ROWS).astype(F32).astype(BF)
        query_list = dot(segs[:ROWS], spread)
        tall = (ROWS, GROUP * ROWS)
        causal = lane(tall, 0) <= lax.rem(lane(tall, 1), ROWS)
        mask[m] = jnp.where((key_list == query_list) & causal, 1.0, 0.0)
    for i in range(D // HF):
        wt[:, i * HF:(i + 1) * HF] = w_ref[i * HF:(i + 1) * HF, :].T
    own = lane((fo, D), 1) == me * fo + lane((fo, D), 0)
    gcol[...] = jnp.sum(jnp.where(own, gain, 0.0), axis=1, keepdims=True)
    gs[...] = jnp.zeros_like(gs)

    listed(0)
    listed(1)

    def probs(m, _):
        allowed = mask[m] > 0.5
        for c in range(KV):
            kc = kl[rows_of(m, ROWS), c * HF:(c + 1) * HF]
            qc = jnp.concatenate(
                [
                    ql[rows_of(m, ROWS), (c * GROUP + h) * HF:(c * GROUP + h + 1) * HF]
                    for h in range(GROUP)
                ],
                axis=0,
            )
            s = dot(kc, qc, NT) * HF ** (-0.5)
            s = jnp.where(allowed, s, MASKED)
            e = jnp.exp(s - jnp.max(s, axis=0, keepdims=True))
            pt[m, c] = (e / jnp.sum(e, axis=0, keepdims=True)).astype(BF)
        return 0

    lax.fori_loop(0, MICRO, probs, 0)

    listed(2)

    def peer(step):
        p = lax.rem(slot + step, slots)
        return p, dev(lax.div(p, 2), my_y, lax.rem(p, 2))

    def columns(p):
        return xl.at[:, pl.ds(pl.multiple_of(p * fw, fw), fw)]

    def x_copy(step):
        p, target = peer(step)
        return remote(columns(p), xs.at[slot], xs_send.at[step], xs_recv, target)

    for step in range(1, slots):
        x_copy(step).start()
    pltpu.make_async_copy(columns(slot), xs.at[slot], xs_recv).start()

    def stats(i, _):
        xf = xl[rows_of(i, PR), :].astype(F32)
        inv[rows_of(i, PR), :] = lax.rsqrt(
            jnp.sum(xf * xf, axis=1, keepdims=True) * (1.0 / D) + EPS
        )
        return 0

    lax.fori_loop(0, PIECES, stats, 0)
    xg = (xl[...].astype(F32) * gain).astype(BF)
    yv[...] = dot(xg, w_ref[...]) * (1.0 / D)

    def turn_x():
        pltpu.make_async_copy(xs, xs, xs_recv).wait()
        for i in range(slots):
            xst[:, i * TOK:(i + 1) * TOK] = xs[i].T

    @pl.when(sec < nz // 2)
    def _():
        turn_x()

    @pl.when(sec == last)
    def _():
        up_copy.wait()

    def g_copy(ci):
        return remote(
            out.at[rows_of(ci, PR), :], gin.at[rows_of(ci, PR), :],
            gout_sem.at[ci], gin_sem.at[ci], me, lax.max(sec - 1, 0),
        )

    def u_copy(ci, step):
        _, target = peer(step)
        rows = us.at[slot, rows_of(ci, PR), :]
        return remote(rows, rows, us_send.at[ci, step], us_recv, target)

    def chain(t, _):
        m = lax.rem(t, MICRO)
        b = PER - 1 - lax.div(t, MICRO)
        ci = m * PER + b

        @pl.when(sec < last)
        def _():
            g_copy(ci).wait_recv()

        g = gin[rows_of(ci, PR), :]
        for h in range(HEADS):
            c, hh = divmod(h, GROUP)
            gs[m, c, pl.ds(pl.multiple_of(hh * ROWS + b * PR, PR), PR), :] = g[:, h * HF:(h + 1) * HF]
        v = jnp.concatenate(
            [dot(pt[m, c, rows_of(b, PR), :], gs[m, c]) for c in range(KV)], axis=1
        ).astype(BF)
        r = inv[rows_of(ci, PR), :]
        uf = v.astype(F32) * r
        u = uf.astype(BF)
        coef = jnp.sum(uf * yv[rows_of(ci, PR), :], axis=1, keepdims=True) * (r * r)
        ng = dot(u, wt[...])
        xf = xl[rows_of(ci, PR), :].astype(F32)
        out[rows_of(ci, PR), :] = (g.astype(F32) + (gain * ng - xf * coef)).astype(BF)
        us[slot, rows_of(ci, PR), :] = u

        @pl.when(sec > 0)
        def _():
            g_copy(ci).start()

        for step in range(1, slots):
            u_copy(ci, step).start()

        def back(i, _):
            target = ci * (PR // pair) + i
            src = out.at[rows_of(target, pair), :]
            dst = fin_ref.at[rows_of(me, pair), :]

            @pl.when(target != me)
            def _():
                remote(src, dst, fin_send, fin_recv, target).start()

            @pl.when(target == me)
            def _():
                pltpu.make_async_copy(src, dst, fin_recv).start()
                pltpu.make_async_copy(src, spare.at[3, pl.ds(0, pair), :], fin_send).start()

            return 0

        lax.fori_loop(0, PR // pair, back, 0)
        return 0

    lax.fori_loop(0, PIECES, chain, 0)

    @pl.when(sec >= nz // 2)
    def _():
        turn_x()

    others = us.at[pl.ds(0, slots - 1)]
    pltpu.make_async_copy(others, others, us_recv).wait()
    acc = dot(xst[...], us[...].reshape(slots * TOK, KW))
    cst[...] = acc.astype(BF).reshape(ny, fo, KW)

    def part_copy(j):
        yl, c = divmod(j, 2)
        target = dev(my_x, core * (ny // 2) + yl, c)
        return target, remote(cst.at[j], part.at[my_y], part_send.at[j], part_recv, target)

    for j in range(ny):
        target, copy = part_copy(j)

        @pl.when(target != me)
        def _():
            copy.start()

        @pl.when(target == me)
        def _():
            pltpu.make_async_copy(cst.at[j], part.at[my_y], part_recv).start()

    pltpu.make_async_copy(part, part, part_recv).wait()
    total = part[0].astype(F32)
    for y in range(1, ny):
        total = total + part[y].astype(F32)
    total = total * scale
    wg_ref[...] = total * gcol[...]
    terms = total * w_ref[rows_of(me, fo), :].astype(F32)
    gg_ref[...] = jnp.sum(terms.T, axis=0, keepdims=True)

    pltpu.make_async_copy(fin_ref, fin_ref, fin_recv).wait()

    pltpu.make_async_copy(out, out, fin_send).wait()
    for n, (_, dst) in enumerate(arrays):
        pltpu.make_async_copy(dst, dst, list_send.at[n]).wait()
    for step in range(1, slots):
        x_copy(step).wait_send()

    def drain(ci, _):
        for step in range(1, slots):
            u_copy(ci, step).wait_send()

        @pl.when(sec > 0)
        def _():
            g_copy(ci).wait_send()

        return 0

    lax.fori_loop(0, PIECES, drain, 0)
    for j in range(ny):
        target, copy = part_copy(j)

        @pl.when(target != me)
        def _():
            copy.wait_send()


def finish(fin_ref, wg_ref, gg_ref, input_ref, weight_ref, gain_ref):
    input_ref[0] = fin_ref[...]
    weight_ref[0] = wg_ref[...]
    gain_ref[...] = gg_ref[...]


def on_device(nx, ny, nz, hidden_in, queries, keys, segments, value_weight, norm_gain, upstream):
    slots = 2 * nx
    ndp = slots * ny
    fw = D // slots
    fo = D // ndp
    pair = TOK // ndp
    vmem = pl.BlockSpec(memory_space=pltpu.VMEM)
    hbm = pl.BlockSpec(memory_space=pl.ANY)
    sem = pltpu.SemaphoreType.DMA
    fin, wg, gg = pl.pallas_call(
        functools.partial(kernel, nx, ny, nz),
        out_shape=(
            jax.ShapeDtypeStruct((TOK, D), BF),
            jax.ShapeDtypeStruct((fo, KW), F32),
            jax.ShapeDtypeStruct((1, fo), F32),
        ),
        in_specs=[hbm] * 3 + [vmem] * 3 + [hbm],
        out_specs=(vmem, vmem, vmem),
        scratch_shapes=[
            pltpu.VMEM((TOK, D), BF),
            pltpu.VMEM((TOK, KW), BF),
            pltpu.VMEM((TOK, D), BF),
            pltpu.VMEM((TOK, D), BF),
            pltpu.VMEM((TOK, D), BF),
            pltpu.VMEM((MICRO, KV, GROUP * ROWS, HF), BF),
            pltpu.VMEM((MICRO, ROWS, GROUP * ROWS), F32),
            pltpu.VMEM((MICRO, KV, ROWS, GROUP * ROWS), BF),
            pltpu.VMEM((TOK, KW), F32),
            pltpu.VMEM((TOK, 1), F32),
            pltpu.VMEM((KW, D), BF),
            pltpu.VMEM((slots, TOK, fw), BF),
            pltpu.VMEM((fw, slots * TOK), BF),
            pltpu.VMEM((slots, TOK, KW), BF),
            pltpu.VMEM((ny, fo, KW), BF),
            pltpu.VMEM((ny, fo, KW), BF),
            pltpu.VMEM((fo, 1), F32),
            pltpu.VMEM((4, max(pair, 16), D), BF),
            sem,
            sem((3,)),
            sem((3,)),
            sem((PIECES,)),
            sem((PIECES,)),
            sem,
            sem,
            sem,
            sem((slots,)),
            sem,
            sem((PIECES, slots)),
            sem,
            sem((ny,)),
        ],
        compiler_params=pltpu.CompilerParams(
            collective_id=0, has_side_effects=True, vmem_limit_bytes=60000 * 1024
        ),
        name="chain",
    )(
        hidden_in[0], queries[0], keys[0], segments, value_weight[0], norm_gain, upstream
    )
    return pl.pallas_call(
        finish,
        out_shape=(
            jax.ShapeDtypeStruct((1, TOK, D), BF),
            jax.ShapeDtypeStruct((1, fo, KW), F32),
            jax.ShapeDtypeStruct((1, fo), F32),
        ),
        in_specs=[vmem] * 3,
        out_specs=(vmem, vmem, vmem),
        name="finish",
    )(fin, wg, gg)


def solution(mesh):
    ndp = mesh.shape["dp"]
    nx = XS
    ny = ndp // (2 * nx)
    in_specs = (
        P("section", "dp", None),
        P("section", "dp", None),
        P("section", "dp", None),
        P("dp", None),
        P("section", None, None),
        P("section", None),
        P("dp", None),
    )
    out_specs = (P("section", "dp", None), P("section", "dp", None), P("section", "dp"))
    return jax.shard_map(
        functools.partial(on_device, nx, ny, mesh.shape["section"]),
        mesh=mesh, in_specs=in_specs, out_specs=out_specs, check_vma=False,
    )
```

```python
import functools

import jax
import jax.numpy as jnp
from jax import lax
from jax.experimental import pallas as pl
from jax.experimental.pallas import tpu as pltpu
from jax.sharding import PartitionSpec as P

HEADS = 16
KV = 4
GROUP = HEADS // KV
HF = 128
D = HEADS * HF
KW = KV * HF
ROWS = 64
MICRO = 2
TOK = ROWS * MICRO
PR = 8
PIECES = TOK // PR
PER = ROWS // PR
EPS = 1e-06
MASKED = -1e30
XS = 4
MESH = pl.DeviceIdType.MESH
F32 = jnp.float32
BF = jnp.bfloat16


def dot(a, b, dims=(((1,), (0,)), ((), ()))):
    return lax.dot_general(a, b, dims, preferred_element_type=F32)


NT = (((1,), (1,)), ((), ()))


def rows_of(i, n):
    return pl.ds(pl.multiple_of(i * n, n), n)


def kernel(
    nx, ny, nz,
    x_in, q_in, k_in, seg_ref, w_in, gain_ref, up_ref,
    fin_ref, wg_ref, gg_ref,
    ql, kl, xl, out, gin, gs, mask, pt, yv, inv, wt, xs, xst, us, cst, part, gcol, spare, w_ref,
    up_sem, w_sem, list_recv, list_send, gin_sem, gout_sem, fin_recv, fin_send,
    xs_recv, xs_send, us_recv, us_send, part_recv, part_send,
):
    me = lax.axis_index("dp")
    sec = lax.axis_index("section")
    core = lax.rem(me, 2)
    my_y = lax.rem(lax.div(me, 2), ny)
    my_x = lax.div(me, 2 * ny)
    last = nz - 1
    ndp = 2 * nx * ny
    pair = TOK // ndp
    slots = 2 * nx
    fw = D // slots
    fo = D // ndp
    slot = my_x * 2 + core
    scale = float(TOK * ndp) ** (-0.5)

    def dev(x, y, c):
        return (x * ny + y) * 2 + c

    def remote(src, dst, send, recv, target, section=None):
        return pltpu.make_async_remote_copy(
            src_ref=src, dst_ref=dst, send_sem=send, recv_sem=recv,
            device_id=(target, sec if section is None else section), device_id_type=MESH,
        )

    barrier = pltpu.get_barrier_semaphore()

    def greet(d, _):
        pl.semaphore_signal(
            barrier, inc=1, device_id=(lax.rem(me + d, ndp), sec), device_id_type=MESH
        )
        return 0

    lax.fori_loop(1, ndp, greet, 0)

    @pl.when(sec > 0)
    def _():
        pl.semaphore_signal(barrier, inc=1, device_id=(me, sec - 1), device_id_type=MESH)

    @pl.when(sec < last)
    def _():
        pl.semaphore_signal(barrier, inc=1, device_id=(me, sec + 1), device_id_type=MESH)

    w_copy = pltpu.make_async_copy(w_in, w_ref, w_sem)
    w_copy.start()
    up_copy = pltpu.make_async_copy(up_ref, gin, up_sem)

    @pl.when(sec == last)
    def _():
        up_copy.start()

    neighbours = (sec > 0).astype(jnp.int32) + (sec < last).astype(jnp.int32)
    pl.semaphore_wait(barrier, ndp - 1 + neighbours)

    arrays = ((k_in, kl), (q_in, ql), (x_in, xl))
    for n, (src, dst) in enumerate(arrays):

        def give(d, _):
            target = lax.rem(me + d, ndp)
            remote(
                src.at[rows_of(target, pair), :], dst.at[rows_of(me, pair), :],
                list_send.at[n], list_recv.at[n], target,
            ).start()
            return 0

        lax.fori_loop(1, ndp, give, 0)
        pltpu.make_async_copy(
            src.at[rows_of(me, pair), :], dst.at[rows_of(me, pair), :], list_recv.at[n]
        ).start()
        pltpu.make_async_copy(
            src.at[rows_of(me, pair), :],
            spare.at[n, pl.ds(0, pair), pl.ds(0, src.shape[1])],
            list_send.at[n],
        ).start()

    def listed(n):
        pltpu.make_async_copy(arrays[n][1], arrays[n][1], list_recv.at[n]).wait()

    gain = gain_ref[...]
    segs = jnp.broadcast_to(seg_ref[...].astype(F32), (GROUP * ROWS, TOK)).astype(BF)

    def lane(shape, axis):
        return lax.broadcasted_iota(jnp.int32, shape, axis)

    for m in range(MICRO):
        pick = (lane((ROWS, TOK), 0) + m * ROWS == lane((ROWS, TOK), 1)).astype(F32).astype(BF)
        key_list = dot(pick, segs, NT)
        wide = (TOK, GROUP * ROWS)
        spread = (lane(wide, 0) == lax.rem(lane(wide, 1), ROWS) + m * ROWS).astype(F32).astype(BF)
        query_list = dot(segs[:ROWS], spread)
        tall = (ROWS, GROUP * ROWS)
        causal = lane(tall, 0) <= lax.rem(lane(tall, 1), ROWS)
        mask[m] = jnp.where((key_list == query_list) & causal, 1.0, 0.0)
    w_copy.wait()
    for i in range(D // HF):
        wt[:, i * HF:(i + 1) * HF] = w_ref[i * HF:(i + 1) * HF, :].T
    own = lane((fo, D), 1) == me * fo + lane((fo, D), 0)
    gcol[...] = jnp.sum(jnp.where(own, gain, 0.0), axis=1, keepdims=True)
    gs[...] = jnp.zeros_like(gs)

    listed(0)
    listed(1)

    def probs(m, _):
        allowed = mask[m] > 0.5
        for c in range(KV):
            kc = kl[rows_of(m, ROWS), c * HF:(c + 1) * HF]
            qc = jnp.concatenate(
                [
                    ql[rows_of(m, ROWS), (c * GROUP + h) * HF:(c * GROUP + h + 1) * HF]
                    for h in range(GROUP)
                ],
                axis=0,
            )
            s = dot(kc, qc, NT) * HF ** (-0.5)
            s = jnp.where(allowed, s, MASKED)
            e = jnp.exp(s - jnp.max(s, axis=0, keepdims=True))
            pt[m, c] = (e / jnp.sum(e, axis=0, keepdims=True)).astype(BF)
        return 0

    lax.fori_loop(0, MICRO, probs, 0)

    listed(2)

    def peer(step):
        p = lax.rem(slot + step, slots)
        return p, dev(lax.div(p, 2), my_y, lax.rem(p, 2))

    def columns(p):
        return xl.at[:, pl.ds(pl.multiple_of(p * fw, fw), fw)]

    def x_copy(step):
        p, target = peer(step)
        return remote(columns(p), xs.at[slot], xs_send.at[step], xs_recv, target)

    for step in range(1, slots):
        x_copy(step).start()
    pltpu.make_async_copy(columns(slot), xs.at[slot], xs_recv).start()

    xf = xl[...].astype(F32)
    inv[...] = lax.rsqrt(jnp.sum(xf * xf, axis=1, keepdims=True) * (1.0 / D) + EPS)
    xg = (xf * gain).astype(BF)
    yv[...] = dot(xg, w_ref[...]) * (1.0 / D)

    def turn_x():
        pltpu.make_async_copy(xs, xs, xs_recv).wait()
        for i in range(slots):
            xst[:, i * TOK:(i + 1) * TOK] = xs[i].T

    @pl.when(sec < nz // 2)
    def _():
        turn_x()

    @pl.when(sec == last)
    def _():
        up_copy.wait()

    def g_copy(ci):
        return remote(
            out.at[rows_of(ci, PR), :], gin.at[rows_of(ci, PR), :],
            gout_sem.at[ci], gin_sem.at[ci], me, lax.max(sec - 1, 0),
        )

    def u_copy(ci, step):
        _, target = peer(step)
        rows = us.at[slot, rows_of(ci, PR), :]
        return remote(rows, rows, us_send.at[ci, step], us_recv, target)

    def chain(t, _):
        m = lax.rem(t, MICRO)
        b = PER - 1 - lax.div(t, MICRO)
        ci = m * PER + b

        @pl.when(sec < last)
        def _():
            g_copy(ci).wait_recv()

        g = gin[rows_of(ci, PR), :]
        for h in range(HEADS):
            c, hh = divmod(h, GROUP)
            gs[m, c, pl.ds(pl.multiple_of(hh * ROWS + b * PR, PR), PR), :] = g[:, h * HF:(h + 1) * HF]
        v = jnp.concatenate(
            [dot(pt[m, c, rows_of(b, PR), :], gs[m, c]) for c in range(KV)], axis=1
        ).astype(BF)
        r = inv[rows_of(ci, PR), :]
        uf = v.astype(F32) * r
        u = uf.astype(BF)
        coef = jnp.sum(uf * yv[rows_of(ci, PR), :], axis=1, keepdims=True) * (r * r)
        ng = dot(u, wt[...])
        xf = xl[rows_of(ci, PR), :].astype(F32)
        out[rows_of(ci, PR), :] = (g.astype(F32) + (gain * ng - xf * coef)).astype(BF)
        us[slot, rows_of(ci, PR), :] = u

        @pl.when(sec > 0)
        def _():
            g_copy(ci).start()

        for step in range(1, slots):
            u_copy(ci, step).start()

        def back(i, _):
            target = ci * (PR // pair) + i
            src = out.at[rows_of(target, pair), :]
            dst = fin_ref.at[rows_of(me, pair), :]

            @pl.when(target != me)
            def _():
                remote(src, dst, fin_send, fin_recv, target).start()

            @pl.when(target == me)
            def _():
                pltpu.make_async_copy(src, dst, fin_recv).start()
                pltpu.make_async_copy(src, spare.at[3, pl.ds(0, pair), :], fin_send).start()

            return 0

        lax.fori_loop(0, PR // pair, back, 0)
        return 0

    lax.fori_loop(0, PIECES, chain, 0)

    @pl.when(sec >= nz // 2)
    def _():
        turn_x()

    others = us.at[pl.ds(0, slots - 1)]
    pltpu.make_async_copy(others, others, us_recv).wait()
    acc = dot(xst[...], us[...].reshape(slots * TOK, KW))
    cst[...] = acc.astype(BF).reshape(ny, fo, KW)

    def part_copy(j):
        yl, c = divmod(j, 2)
        target = dev(my_x, core * (ny // 2) + yl, c)
        return target, remote(cst.at[j], part.at[my_y], part_send.at[j], part_recv, target)

    for j in range(ny):
        target, copy = part_copy(j)

        @pl.when(target != me)
        def _():
            copy.start()

        @pl.when(target == me)
        def _():
            pltpu.make_async_copy(cst.at[j], part.at[my_y], part_recv).start()

    pltpu.make_async_copy(part, part, part_recv).wait()
    total = part[0].astype(F32)
    for y in range(1, ny):
        total = total + part[y].astype(F32)
    total = total * scale
    wg_ref[...] = total * gcol[...]
    terms = total * w_ref[rows_of(me, fo), :].astype(F32)
    gg_ref[...] = jnp.sum(terms.T, axis=0, keepdims=True)

    pltpu.make_async_copy(fin_ref, fin_ref, fin_recv).wait()

    pltpu.make_async_copy(out, out, fin_send).wait()
    for n, (_, dst) in enumerate(arrays):
        pltpu.make_async_copy(dst, dst, list_send.at[n]).wait()
    for step in range(1, slots):
        x_copy(step).wait_send()

    def drain(ci, _):
        for step in range(1, slots):
            u_copy(ci, step).wait_send()

        @pl.when(sec > 0)
        def _():
            g_copy(ci).wait_send()

        return 0

    lax.fori_loop(0, PIECES, drain, 0)
    for j in range(ny):
        target, copy = part_copy(j)

        @pl.when(target != me)
        def _():
            copy.wait_send()


def finish(fin_ref, wg_ref, gg_ref, input_ref, weight_ref, gain_ref):
    input_ref[0] = fin_ref[...]
    weight_ref[0] = wg_ref[...]
    gain_ref[...] = gg_ref[...]


def on_device(nx, ny, nz, hidden_in, queries, keys, segments, value_weight, norm_gain, upstream):
    slots = 2 * nx
    ndp = slots * ny
    fw = D // slots
    fo = D // ndp
    pair = TOK // ndp
    vmem = pl.BlockSpec(memory_space=pltpu.VMEM)
    hbm = pl.BlockSpec(memory_space=pl.ANY)
    sem = pltpu.SemaphoreType.DMA
    fin, wg, gg = pl.pallas_call(
        functools.partial(kernel, nx, ny, nz),
        out_shape=(
            jax.ShapeDtypeStruct((TOK, D), BF),
            jax.ShapeDtypeStruct((fo, KW), F32),
            jax.ShapeDtypeStruct((1, fo), F32),
        ),
        in_specs=[hbm] * 3 + [vmem, hbm, vmem, hbm],
        out_specs=(vmem, vmem, vmem),
        scratch_shapes=[
            pltpu.VMEM((TOK, D), BF),
            pltpu.VMEM((TOK, KW), BF),
            pltpu.VMEM((TOK, D), BF),
            pltpu.VMEM((TOK, D), BF),
            pltpu.VMEM((TOK, D), BF),
            pltpu.VMEM((MICRO, KV, GROUP * ROWS, HF), BF),
            pltpu.VMEM((MICRO, ROWS, GROUP * ROWS), F32),
            pltpu.VMEM((MICRO, KV, ROWS, GROUP * ROWS), BF),
            pltpu.VMEM((TOK, KW), F32),
            pltpu.VMEM((TOK, 1), F32),
            pltpu.VMEM((KW, D), BF),
            pltpu.VMEM((slots, TOK, fw), BF),
            pltpu.VMEM((fw, slots * TOK), BF),
            pltpu.VMEM((slots, TOK, KW), BF),
            pltpu.VMEM((ny, fo, KW), BF),
            pltpu.VMEM((ny, fo, KW), BF),
            pltpu.VMEM((fo, 1), F32),
            pltpu.VMEM((4, max(pair, 16), D), BF),
            pltpu.VMEM((D, KW), BF),
            sem,
            sem,
            sem((3,)),
            sem((3,)),
            sem((PIECES,)),
            sem((PIECES,)),
            sem,
            sem,
            sem,
            sem((slots,)),
            sem,
            sem((PIECES, slots)),
            sem,
            sem((ny,)),
        ],
        compiler_params=pltpu.CompilerParams(
            collective_id=0, has_side_effects=True, vmem_limit_bytes=60000 * 1024
        ),
        name="chain",
    )(
        hidden_in[0], queries[0], keys[0], segments, value_weight[0], norm_gain, upstream
    )
    return pl.pallas_call(
        finish,
        out_shape=(
            jax.ShapeDtypeStruct((1, TOK, D), BF),
            jax.ShapeDtypeStruct((1, fo, KW), F32),
            jax.ShapeDtypeStruct((1, fo), F32),
        ),
        in_specs=[vmem] * 3,
        out_specs=(vmem, vmem, vmem),
        name="finish",
    )(fin, wg, gg)


def solution(mesh):
    ndp = mesh.shape["dp"]
    nx = XS
    ny = ndp // (2 * nx)
    in_specs = (
        P("section", "dp", None),
        P("section", "dp", None),
        P("section", "dp", None),
        P("dp", None),
        P("section", None, None),
        P("section", None),
        P("dp", None),
    )
    out_specs = (P("section", "dp", None), P("section", "dp", None), P("section", "dp"))
    return jax.shard_map(
        functools.partial(on_device, nx, ny, mesh.shape["section"]),
        mesh=mesh, in_specs=in_specs, out_specs=out_specs, check_vma=False,
    )
```
